128 devices in a mesh: wave: 8 (over x, core), deg: 16 (over z, y).
Axes of the slice: x: 4, y: 4, z: 4, core: 2. Of those that a mesh axis runs over, the one named last changes fastest.
Arguments:
- spectrum: bfloat16 [512, 2, 32, 4096], P('wave', None, None, 'deg'), may hold values from -2 to 2
- leaf_map: bfloat16 [512, 4096, 128], P('wave', 'deg'), may hold values from -0.375 to 0.375
- level_maps: bfloat16 [3, 512, 2048, 128], P(None, 'wave', 'deg'), may hold values from -0.5 to 0.5
- lat_map: bfloat16 [512, 128, 2048], P('wave', None, 'deg'), may hold values from -0.0234375 to 0.0234375
- skeleton: int32 [512, 2048], P('wave', 'deg'), may hold values from 0 to 255
- wavemap: int32 [512], replicated, may hold values from 0 to 4095, as said below
Outputs:
- grid: bfloat16 [32, 2048, 8192], P('wave', 'deg')
The draws below stay inside these ranges and needn't reach their ends.
Inputs may be any that keep to these rules, and one draw needn't show every extreme that they name: `skeleton`: for slot m and block b, entries b * 128 to b * 128 + 127 are degrees counted from the first degree of block b. `wavemap`: no two slots hold the same wavenumber.
All inputs are finite; a program needn't handle non-finite values.
Results may differ from the reference program's by a relative error of at most 0.0086.
Values may be sent and summed in bfloat16 or wider, within the bound.
A program may use at most 128 MiB of HBM per device.

```python
import jax
import jax.numpy as jnp
from jax import lax

FL = 32
NODE = 128
NB = 256
WAVE_DEV = 64
WAVES = 512
LEVELS = 3
NLON = 8192
LONG_SPLIT = 32
DEGS = 4096
NLAT = 2048
N_WAVE = 8
N_DEG = 16


def draw_wavemap(key, part):
    half = NLON // 2
    inner = jax.random.permutation(jax.random.fold_in(key, 17), half - 2) + 1
    chosen = jnp.concatenate([jnp.array([0, half - 1], jnp.int32), inner[:WAVES - 2].astype(jnp.int32)])
    ordered = jnp.sort(chosen)
    rank_idx = jnp.arange(WAVES, dtype=jnp.int32)
    phase = rank_idx % (2 * N_WAVE)
    group = jnp.where(phase < N_WAVE, phase, 2 * N_WAVE - 1 - phase)
    slot = group * WAVE_DEV + rank_idx // N_WAVE
    return jnp.zeros((WAVES,), jnp.int32).at[slot].set(ordered)


def place_ends(values, stream_key, least, largest):
    longest = values.shape.index(max(values.shape))
    spots = []
    for shift in (0, 1):
        where = [jax.random.randint(jax.random.fold_in(stream_key, axis), (), 0, length) for axis, length in enumerate(values.shape)]
        where[longest] = (where[longest] + shift) % values.shape[longest]
        spots.append(tuple(where))
    return values.at[spots[0]].set(least).at[spots[1]].set(largest)


def levels(key, extent, shards, smallest, high):
    gain, own = 1.0, jax.random.fold_in(key, 6)
    for axis_at, parts in shards:
        heights = jnp.exp(jax.random.uniform(jax.random.fold_in(own, axis_at), (parts,), jnp.float32, smallest / len(shards), high / len(shards)))
        gain = gain * jnp.repeat(heights, extent[axis_at] // parts).reshape([-1 if axis == axis_at else 1 for axis in range(len(extent))])
    return gain


def bell_draw(rng, shape, width, bound, cuts=(), kind=jnp.bfloat16):
    entries = jax.random.normal(rng, shape, jnp.float32) * width
    if len(cuts) > 0:
        entries = levels(rng, shape, cuts, -0.22, 0.18) * entries
    return jnp.clip(entries, min=-bound, max=bound).astype(kind)


def setup_inputs(seed: int = 0) -> dict:
    splits = jax.random.split(jax.random.key(seed), 7)
    return {
        "spectrum": bell_draw(splits[0], (WAVES, 2, FL, DEGS), 0.35, 2.0, ((0, 8), (3, 16))),
        "leaf_map": bell_draw(splits[1], (WAVES, DEGS, NODE), NB ** -0.5, 0.375, ((0, 8), (1, 16))),
        "level_maps": bell_draw(splits[2], (LEVELS, WAVES, N_DEG * NODE, NODE), NODE ** -0.5, 0.5, ((1, 8), (2, 16))),
        "lat_map": bell_draw(splits[3], (WAVES, NODE, NLAT), (NODE * WAVES) ** -0.5, 0.0234375, ((0, 8), (2, 16))),
        "skeleton": place_ends(jax.random.randint(splits[4], (WAVES, N_DEG * NODE), 0, NB), jax.random.fold_in(splits[4], 1), 0, NB - 1).astype(jnp.int32),
        "wavemap": draw_wavemap(jax.random.fold_in(splits[6], 71), 0),
    }


def long_tables(lon_count, first):
    half = lon_count // 2
    second = half // first
    a_idx = lax.broadcasted_iota(jnp.int32, (first, 2 * first), 0)
    u_idx = lax.broadcasted_iota(jnp.int32, (first, 2 * first), 1)
    ang1 = ((a_idx * u_idx) % (2 * first)).astype(jnp.float32) * (2.0 * jnp.pi / (2 * first))
    cos1 = jnp.cos(ang1)
    sin1 = jnp.sin(ang1)
    table1 = jnp.stack([jnp.stack([cos1, sin1], 1), jnp.stack([-sin1, cos1], 1)], 0).astype(jnp.bfloat16)
    e_idx = lax.broadcasted_iota(jnp.int32, (second, 2 * first), 0)
    w_idx = lax.broadcasted_iota(jnp.int32, (second, 2 * first), 1)
    ang_tw = ((e_idx * w_idx) % lon_count).astype(jnp.float32) * (2.0 * jnp.pi / lon_count)
    tw_cos = jnp.cos(ang_tw)
    tw_sin = jnp.sin(ang_tw)
    e2_idx = lax.broadcasted_iota(jnp.int32, (second, second), 0)
    v_idx = lax.broadcasted_iota(jnp.int32, (second, second), 1)
    ang2 = ((e2_idx * v_idx) % second).astype(jnp.float32) * (2.0 * jnp.pi / second)
    table2 = jnp.stack([jnp.cos(ang2), -jnp.sin(ang2)]).astype(jnp.bfloat16)
    return table1, tw_cos, tw_sin, table2


def long_synthesis(block, wavemap, lon_count, first):
    table1, tw_cos, tw_sin, table2 = long_tables(lon_count, first)
    half = lon_count // 2
    second = half // first
    field_count = block.shape[2]
    row_count = block.shape[3]
    weight = jnp.where(wavemap == 0, 1.0, 2.0).astype(jnp.float32)[:, None, None, None]
    scaled = (weight * block.astype(jnp.float32)).astype(jnp.bfloat16)
    coeffs = jnp.zeros((half, 2, field_count, row_count), jnp.bfloat16).at[wavemap.astype(jnp.int32)].set(scaled)
    coeffs = coeffs.reshape(first, second, 2, field_count, row_count)
    section = jnp.einsum("aerfl,rapu->epufl", coeffs.astype(jnp.float32), table1.astype(jnp.float32))
    real_part = section[:, 0]
    imag_part = section[:, 1]
    tc = tw_cos[:, :, None, None]
    ts = tw_sin[:, :, None, None]
    twisted = jnp.stack([real_part * tc - imag_part * ts, real_part * ts + imag_part * tc], 1).astype(jnp.bfloat16)
    result = jnp.einsum("epufl,pev->flvu", twisted.astype(jnp.float32), table2.astype(jnp.float32))
    return result.reshape(field_count, row_count, lon_count).astype(jnp.bfloat16)


def one_slot(spec_slot, leaf_slot, levels_slot, lat_slot, skel_slot):
    field_count = spec_slot.shape[1]
    columns = 2 * field_count
    flat_coef = spec_slot.reshape(columns, N_DEG, -1).transpose(1, 0, 2)
    node_width = leaf_slot.shape[1]
    half_width = node_width // 2
    skel_index = jnp.broadcast_to(skel_slot.reshape(N_DEG, 1, node_width), (N_DEG, columns, node_width))
    picked = jnp.take_along_axis(flat_coef, skel_index, axis=2)
    leaf_rows = leaf_slot.reshape(N_DEG, -1, node_width)
    node_state = (picked.astype(jnp.float32) + jnp.einsum("bcn,bnk->bck", flat_coef.astype(jnp.float32), leaf_rows.astype(jnp.float32))).astype(jnp.bfloat16)
    blocks = jnp.arange(N_DEG, dtype=jnp.int32)
    for level_num in range(LEVELS):
        low_block = blocks - (blocks & (1 << level_num))
        high_block = low_block + (1 << level_num)
        upper_bit = ((blocks >> level_num) & 1)[:, None, None]
        low_side = node_state[low_block]
        high_side = node_state[high_block]
        low_half = jnp.where(upper_bit == 0, low_side[:, :, :half_width], low_side[:, :, half_width:])
        high_half = jnp.where(upper_bit == 0, high_side[:, :, :half_width], high_side[:, :, half_width:])
        joined = jnp.concatenate([low_half, high_half], axis=2)
        factor = levels_slot[level_num].reshape(N_DEG, node_width, node_width)
        node_state = jnp.einsum("bck,bks->bcs", joined.astype(jnp.float32), factor.astype(jnp.float32)).astype(jnp.bfloat16)
    lat_rows = lat_slot.reshape(node_width, N_DEG, -1)
    lat_values = jnp.einsum("bck,kbl->cbl", node_state.astype(jnp.float32), lat_rows.astype(jnp.float32)).astype(jnp.bfloat16)
    return lat_values.reshape(columns, -1)


def reference(spectrum, leaf_map, level_maps, lat_map, skeleton, wavemap):
    slot_total = spectrum.shape[0]
    field_count = spectrum.shape[2]

    def per_slot(slot):
        return one_slot(spectrum[slot], leaf_map[slot], level_maps[:, slot], lat_map[slot], skeleton[slot])

    lat_values = lax.map(per_slot, jnp.arange(slot_total, dtype=jnp.int32))
    split_values = lat_values.reshape(slot_total, 2, field_count, -1)

    def per_field(field_num):
        chosen = lax.dynamic_slice_in_dim(split_values, field_num, 1, 2)
        return long_synthesis(chosen, wavemap, NLON, LONG_SPLIT)[0]

    return lax.map(per_field, jnp.arange(field_count, dtype=jnp.int32))
```

```python
import functools

import jax
import jax.numpy as jnp
from jax import lax
from jax.experimental import pallas as pl
from jax.experimental.pallas import tpu as pltpu
from jax.sharding import PartitionSpec as P

NLON = 8192
LEVELS = 3
SLOTS = 64
CHUNK = 8
CHUNKS = SLOTS // CHUNK
PAIRS = CHUNK // 2
COLS = 64
NODE = 128
WAVE = 8
LON_TILE = 256
LON_TILES = NLON // LON_TILE
MESH = pl.DeviceIdType.MESH
DELAY = (2, 1, 1, 1)


def comm_kernel(
    spec_hbm, leaf_hbm, lev_hbm, lat_hbm, skel_ref, wm_ref,
    xt_ref, t_hbm,
    spec_v, leaf_v, lev_v, lat_v, state, send, recv, lat32, a_send, a_recv, t_v, q_v,
    spec_sem, leaf_sem, lev_sem, lat_sem, t_sem, l_ssem, l_rsem, a_ssem, a_rsem,
):
    me_w = lax.axis_index("wave")
    me_d = lax.axis_index("deg")
    lane_half = lax.broadcasted_iota(jnp.int32, (COLS, NODE), 1) // (NODE // 2)

    def spec_load(c):
        rows = pl.ds(c * CHUNK, CHUNK)
        return pltpu.make_async_copy(spec_hbm.at[rows], spec_v.at[rows], spec_sem.at[c])

    def leaf_load(c):
        rows = pl.ds(c * CHUNK, CHUNK)
        return pltpu.make_async_copy(leaf_hbm.at[rows], leaf_v.at[rows], leaf_sem.at[c])

    def lev_load(l):
        return pltpu.make_async_copy(lev_hbm.at[l], lev_v.at[l], lev_sem.at[l])

    def lat_load():
        return pltpu.make_async_copy(lat_hbm, lat_v, lat_sem.at[0])

    def t_store(c):
        rows = pl.ds(pl.multiple_of(c * 128, 128), 128)
        return pltpu.make_async_copy(t_v.at[:, rows, :], t_hbm.at[:, rows, :], t_sem.at[c])

    def level_copy(l, c):
        rows = pl.ds(c * PAIRS, PAIRS)
        return pltpu.make_async_remote_copy(
            src_ref=send.at[l, rows],
            dst_ref=recv.at[l, rows],
            send_sem=l_ssem.at[l, c],
            recv_sem=l_rsem.at[l, c],
            device_id={"deg": me_d ^ (1 << l)},
            device_id_type=MESH,
        )

    def wave_copy(c, d, arriving=False):
        target = lax.rem(me_w + d, WAVE)
        place = lax.rem(me_w + WAVE - d, WAVE) if arriving else me_w
        return pltpu.make_async_remote_copy(
            src_ref=a_send.at[c, target],
            dst_ref=a_recv.at[c, place],
            send_sem=a_ssem.at[c, d - 1],
            recv_sem=a_rsem.at[c, d - 1],
            device_id={"wave": target},
            device_id_type=MESH,
        )

    for c in range(CHUNKS):
        spec_load(c).start()
        leaf_load(c).start()
    for l in range(LEVELS):
        lev_load(l).start()
    lat_load().start()

    barrier = pltpu.get_barrier_semaphore()
    for l in range(LEVELS):
        pl.semaphore_signal(barrier, inc=1, device_id={"deg": me_d ^ (1 << l)}, device_id_type=MESH)
    for d in range(1, WAVE):
        pl.semaphore_signal(
            barrier, inc=1, device_id={"wave": lax.rem(me_w + d, WAVE)}, device_id_type=MESH
        )

    def pack(l, c):
        s = lax.rem(me_d // (1 << l), 2)
        mask = lane_half == 1 - s
        for p in range(PAIRS):
            base = c * CHUNK + 2 * p
            kept = state[base + 1 - s]
            moved = pltpu.roll(state[base + s], NODE // 2, 1)
            send[l, c * PAIRS + p] = jnp.where(mask, kept, moved)

    def leaf(c):
        spec_load(c).wait()
        leaf_load(c).wait()
        degree = lax.broadcasted_iota(jnp.int32, (256, NODE), 0)
        for j in range(CHUNK):
            m = c * CHUNK + j
            coef = spec_v[m]
            picks = jnp.where(degree == skel_ref[pl.ds(m, 1), :], 1.0, 0.0).astype(jnp.bfloat16)
            acc = jnp.dot(coef, picks, preferred_element_type=jnp.float32)
            acc = acc + jnp.dot(coef, leaf_v[m], preferred_element_type=jnp.float32)
            state[m] = acc.astype(jnp.bfloat16)
        pack(0, c)

    def combine(l, c):
        level_copy(l, c).wait_recv()
        s = lax.rem(me_d // (1 << l), 2)
        mask = lane_half == s
        for p in range(PAIRS):
            base = c * CHUNK + 2 * p
            got = recv[l, c * PAIRS + p]
            turned = pltpu.roll(got, NODE // 2, 1)
            for m, other in ((base + 1 - s, got), (base + s, turned)):
                joined = jnp.where(mask, state[m], other)
                state[m] = jnp.dot(
                    joined, lev_v[l, m], preferred_element_type=jnp.float32
                ).astype(jnp.bfloat16)

    def latitudes(c):
        for j in range(CHUNK):
            m = c * CHUNK + j
            rows = jnp.dot(state[m], lat_v[m], preferred_element_type=jnp.float32)
            for r in range(2):
                lat32[pl.ds(r * CHUNK + j, 32, stride=2 * CHUNK), :] = rows[r * 32 : (r + 1) * 32]
        for w in range(WAVE):
            a_send[c, w] = lat32[w * 64 : (w + 1) * 64, :].astype(jnp.bfloat16)
        a_recv[c, me_w] = a_send[c, me_w]
        for d in range(1, WAVE):
            wave_copy(c, d).start()

    def gathered(c):
        for d in range(1, WAVE):
            wave_copy(c, d, True).wait_recv()
        for f in range(4):
            block = a_recv[c, :, f * 16 : (f + 1) * 16, :].reshape(NODE, 128)
            xt_ref[f * 128 : (f + 1) * 128, pl.ds(pl.multiple_of(c * 128, 128), 128)] = (
                block.astype(jnp.float32).T.astype(jnp.bfloat16)
            )

    def table(c):
        lanes = lax.broadcasted_iota(jnp.int32, (CHUNK, 128), 1)
        unit = 2.0 * jnp.pi / NLON
        start, turn = [], []
        for w in range(WAVE):
            q = q_v[pl.ds(pl.multiple_of(w * SLOTS + c * CHUNK, 8), CHUNK), :]
            weight = jnp.where(q == 0.0, 1.0, 2.0)
            qi = q.astype(jnp.int32)
            first = lax.rem(qi * lanes, NLON).astype(jnp.float32) * unit
            step = lax.rem(qi * 128, NLON).astype(jnp.float32) * unit
            start += [weight * jnp.cos(first), -weight * jnp.sin(first)]
            turn += [jnp.cos(step), jnp.sin(step)]

        def tile(t, carry):
            carry = list(carry)
            for half in range(2):
                for w in range(WAVE):
                    co, si = carry[2 * w], carry[2 * w + 1]
                    rc, rs = turn[2 * w], turn[2 * w + 1]
                    rows = pl.ds(pl.multiple_of(c * 128 + w * 16, 16), 16)
                    t_v[t, rows, half * 128 : (half + 1) * 128] = jnp.concatenate(
                        [co, si], axis=0
                    ).astype(jnp.bfloat16)
                    carry[2 * w] = co * rc + si * rs
                    carry[2 * w + 1] = si * rc - co * rs
            return tuple(carry)

        lax.fori_loop(0, LON_TILES, tile, tuple(start))
        t_store(c).start()

    leaf(0)
    for g in range(4):
        row = wm_ref[g : g + 1, :].astype(jnp.float32)
        q_v[g * 128 : (g + 1) * 128, :] = jnp.broadcast_to(row, (128, 128)).T
    pl.semaphore_wait(barrier, LEVELS + WAVE - 1)
    level_copy(0, 0).start()

    offsets = [0]
    for d in DELAY:
        offsets.append(offsets[-1] + d)

    def active(t, k):
        return jnp.logical_and(t >= offsets[k], t < offsets[k] + CHUNKS)

    def step(t, _):
        @pl.when(jnp.logical_and(t >= 1, t < CHUNKS))
        def _():
            leaf(t)
            level_copy(0, t).start()

        @pl.when(active(t, 1))
        def _():
            c = t - offsets[1]

            @pl.when(c == 0)
            def _():
                lev_load(0).wait()

            combine(0, c)
            pack(1, c)
            level_copy(1, c).start()

        @pl.when(active(t, 2))
        def _():
            c = t - offsets[2]

            @pl.when(c == 0)
            def _():
                lev_load(1).wait()

            combine(1, c)
            pack(2, c)
            level_copy(2, c).start()

        @pl.when(active(t, 3))
        def _():
            c = t - offsets[3]

            @pl.when(c == 0)
            def _():
                lev_load(2).wait()
                lat_load().wait()

            combine(2, c)
            latitudes(c)

        @pl.when(active(t, 4))
        def _():
            gathered(t - offsets[4])

        @pl.when(t < CHUNKS)
        def _():
            table(t)

        return 0

    lax.fori_loop(0, CHUNKS + offsets[4], step, 0)

    def drain(c, _):
        for l in range(LEVELS):
            level_copy(l, c).wait_send()
        for d in range(1, WAVE):
            wave_copy(c, d).wait_send()
        t_store(c).wait()
        return 0

    lax.fori_loop(0, CHUNKS, drain, 0)


def dft_kernel(tiles, xt_ref, t_ref, out_ref):
    for b in range(tiles):
        out_ref[:, b * LON_TILE : (b + 1) * LON_TILE] = jnp.dot(
            xt_ref[...], t_ref[b], preferred_element_type=jnp.float32
        ).astype(jnp.bfloat16)


def body(spectrum, leaf_map, level_maps, lat_map, skeleton, wavemap):
    any_spec = pl.BlockSpec(memory_space=pl.ANY)
    vmem_spec = pl.BlockSpec(memory_space=pltpu.VMEM)
    bf16, f32 = jnp.bfloat16, jnp.float32
    dma = pltpu.SemaphoreType.DMA
    xt, table = pl.pallas_call(
        comm_kernel,
        out_shape=(
            jax.ShapeDtypeStruct((512, 1024), bf16),
            jax.ShapeDtypeStruct((LON_TILES, 1024, LON_TILE), bf16),
        ),
        in_specs=[any_spec] * 4 + [vmem_spec] * 2,
        out_specs=(vmem_spec, any_spec),
        scratch_shapes=[
            pltpu.VMEM((SLOTS, COLS, 256), bf16),
            pltpu.VMEM((SLOTS, 256, NODE), bf16),
            pltpu.VMEM((LEVELS, SLOTS, NODE, NODE), bf16),
            pltpu.VMEM((SLOTS, NODE, NODE), bf16),
            pltpu.VMEM((SLOTS, COLS, NODE), bf16),
            pltpu.VMEM((LEVELS, SLOTS // 2, COLS, NODE), bf16),
            pltpu.VMEM((LEVELS, SLOTS // 2, COLS, NODE), bf16),
            pltpu.VMEM((CHUNK * COLS, NODE), f32),
            pltpu.VMEM((CHUNKS, WAVE, 64, NODE), bf16),
            pltpu.VMEM((CHUNKS, WAVE, 64, NODE), bf16),
            pltpu.VMEM((LON_TILES, 1024, LON_TILE), bf16),
            pltpu.VMEM((512, 128), f32),
            dma((CHUNKS,)),
            dma((CHUNKS,)),
            dma((LEVELS,)),
            dma((1,)),
            dma((CHUNKS,)),
            dma((LEVELS, CHUNKS)),
            dma((LEVELS, CHUNKS)),
            dma((CHUNKS, WAVE - 1)),
            dma((CHUNKS, WAVE - 1)),
        ],
        compiler_params=pltpu.CompilerParams(
            collective_id=0, has_side_effects=True, vmem_limit_bytes=60 * 1024 * 1024
        ),
    )(
        spectrum.reshape(SLOTS, COLS, 256),
        leaf_map,
        level_maps,
        lat_map,
        skeleton,
        wavemap.reshape(4, 128),
    )
    tiles = 2
    grid = pl.pallas_call(
        functools.partial(dft_kernel, tiles),
        out_shape=jax.ShapeDtypeStruct((512, NLON), bf16),
        grid=(LON_TILES // tiles,),
        in_specs=[
            pl.BlockSpec((512, 1024), lambda i: (0, 0)),
            pl.BlockSpec((tiles, 1024, LON_TILE), lambda i: (i, 0, 0)),
        ],
        out_specs=pl.BlockSpec((512, tiles * LON_TILE), lambda i: (0, i)),
        compiler_params=pltpu.CompilerParams(
            dimension_semantics=("arbitrary",), vmem_limit_bytes=32 * 1024 * 1024
        ),
    )(xt, table)
    return grid.reshape(4, 128, NLON)


def solution(mesh):
    placed = (
        P("wave", None, None, "deg"),
        P("wave", "deg", None),
        P(None, "wave", "deg", None),
        P("wave", None, "deg"),
        P("wave", "deg"),
        P(),
    )
    return jax.shard_map(
        body, mesh=mesh, in_specs=placed, out_specs=P("wave", "deg", None), check_vma=False
    )
```

```python
import jax
import jax.numpy as jnp
from jax import lax
from jax.experimental import pallas as pl
from jax.experimental.pallas import tpu as pltpu
from jax.sharding import PartitionSpec as P

NLON = 8192
LEVELS = 3
SLOTS = 64
CHUNK = 8
CHUNKS = SLOTS // CHUNK
PAIRS = CHUNK // 2
COLS = 64
NODE = 128
WAVE = 8
LON_TILE = 256
LON_TILES = NLON // 2 // LON_TILE
MESH = pl.DeviceIdType.MESH
DELAY = (3, 3, 2, 2)
UNROLL = 4
VMEM_FIRST = 54
VMEM_SECOND = 16


def comm_kernel(
    spec_hbm, leaf_hbm, lev_hbm, lat_hbm, skel_ref, wm_ref,
    xt_ref, t_ref,
    spec_v, leaf_v, lev_v, lat_v, state, send, recv, lat32, a_send, a_recv, q_v, ph_c, ph_s,
    spec_sem, leaf_sem, lev_sem, lat_sem, l_ssem, l_rsem, a_ssem, a_rsem,
):
    me_w = lax.axis_index("wave")
    me_d = lax.axis_index("deg")
    lane_half = lax.broadcasted_iota(jnp.int32, (COLS, NODE), 1) // (NODE // 2)

    def spec_load(c):
        rows = pl.ds(c * CHUNK, CHUNK)
        return pltpu.make_async_copy(spec_hbm.at[rows], spec_v.at[rows], spec_sem.at[c])

    def leaf_load(c):
        rows = pl.ds(c * CHUNK, CHUNK)
        return pltpu.make_async_copy(leaf_hbm.at[rows], leaf_v.at[rows], leaf_sem.at[c])

    def lev_load(l):
        return pltpu.make_async_copy(lev_hbm.at[l], lev_v.at[l], lev_sem.at[l])

    def lat_load():
        return pltpu.make_async_copy(lat_hbm, lat_v, lat_sem.at[0])

    def level_copy(l, c):
        rows = pl.ds(c * PAIRS, PAIRS)
        return pltpu.make_async_remote_copy(
            src_ref=send.at[l, rows],
            dst_ref=recv.at[l, rows],
            send_sem=l_ssem.at[l, c],
            recv_sem=l_rsem.at[l, c],
            device_id={"deg": me_d ^ (1 << l)},
            device_id_type=MESH,
        )

    def wave_copy(c, d, arriving=False):
        target = lax.rem(me_w + d, WAVE)
        place = lax.rem(me_w + WAVE - d, WAVE) if arriving else me_w
        return pltpu.make_async_remote_copy(
            src_ref=a_send.at[c, target],
            dst_ref=a_recv.at[c, place],
            send_sem=a_ssem.at[c, d - 1],
            recv_sem=a_rsem.at[c, d - 1],
            device_id={"wave": target},
            device_id_type=MESH,
        )

    for c in range(CHUNKS):
        spec_load(c).start()
        leaf_load(c).start()
    for l in range(LEVELS):
        lev_load(l).start()
    lat_load().start()

    barrier = pltpu.get_barrier_semaphore()
    for l in range(LEVELS):
        pl.semaphore_signal(barrier, inc=1, device_id={"deg": me_d ^ (1 << l)}, device_id_type=MESH)
    for d in range(1, WAVE):
        pl.semaphore_signal(
            barrier, inc=1, device_id={"wave": lax.rem(me_w + d, WAVE)}, device_id_type=MESH
        )

    def pack(l, c, values):
        s = lax.rem(me_d // (1 << l), 2)
        mask = lane_half == 1 - s
        upper = jnp.broadcast_to(s, (COLS, NODE)) == 1
        for p in range(PAIRS):
            even, odd = values[2 * p], values[2 * p + 1]
            kept = jnp.where(upper, even, odd)
            moved = pltpu.roll(jnp.where(upper, odd, even), NODE // 2, 1)
            send[l, c * PAIRS + p] = jnp.where(mask, kept, moved)

    def leaf(c):
        spec_load(c).wait()
        leaf_load(c).wait()
        degree = lax.broadcasted_iota(jnp.int32, (256, NODE), 0)
        values = []
        for j in range(CHUNK):
            m = c * CHUNK + j
            coef = spec_v[m]
            picks = jnp.where(degree == skel_ref[pl.ds(m, 1), :], 1.0, 0.0).astype(jnp.bfloat16)
            acc = jnp.dot(coef, picks, preferred_element_type=jnp.float32)
            acc = acc + jnp.dot(coef, leaf_v[m], preferred_element_type=jnp.float32)
            values.append(acc.astype(jnp.bfloat16))
        for j in range(CHUNK):
            state[c * CHUNK + j] = values[j]
        pack(0, c, values)

    def combine(l, c):
        level_copy(l, c).wait_recv()
        s = lax.rem(me_d // (1 << l), 2)
        mask = lane_half == s
        upper = jnp.broadcast_to(s, (COLS, NODE)) == 1
        joined = []
        for p in range(PAIRS):
            got = recv[l, c * PAIRS + p]
            turned = pltpu.roll(got, NODE // 2, 1)
            for j, other in (
                (2 * p, jnp.where(upper, got, turned)),
                (2 * p + 1, jnp.where(upper, turned, got)),
            ):
                joined.append(jnp.where(mask, state[c * CHUNK + j], other))
        values = [
            jnp.dot(joined[j], lev_v[l, c * CHUNK + j], preferred_element_type=jnp.float32).astype(
                jnp.bfloat16
            )
            for j in range(CHUNK)
        ]
        if l < LEVELS - 1:
            for j in range(CHUNK):
                state[c * CHUNK + j] = values[j]
            pack(l + 1, c, values)
        return values

    def latitudes(c, values):
        for j in range(CHUNK):
            rows = jnp.dot(values[j], lat_v[c * CHUNK + j], preferred_element_type=jnp.float32)
            real, imag = rows[:32], rows[32:]
            at = pl.ds(c * CHUNK + j, 1)
            co, si = ph_c[at, :], ph_s[at, :]
            lat32[pl.ds(j, 32, stride=2 * CHUNK), :] = real * co + imag * si
            lat32[pl.ds(CHUNK + j, 32, stride=2 * CHUNK), :] = imag * co - real * si
        for w in range(WAVE):
            a_send[c, w] = lat32[w * 64 : (w + 1) * 64, :].astype(jnp.bfloat16)
        a_recv[c, me_w] = a_send[c, me_w]
        for d in range(1, WAVE):
            wave_copy(c, d).start()

    def gathered(pair):
        for k in range(2):
            for d in range(1, WAVE):
                wave_copy(2 * pair + k, d, True).wait_recv()
        lanes = pl.ds(pl.multiple_of(pair * 128, 128), 128)
        for f in range(4):
            block = jnp.concatenate(
                [
                    a_recv[2 * pair + k, :, f * 16 : (f + 1) * 16, :].astype(jnp.float32)
                    for k in range(2)
                ],
                axis=0,
            )
            for r in range(2):
                part = block[:, r * 8 : (r + 1) * 8, :].reshape(128, 128)
                xt_ref[r, f * 128 : (f + 1) * 128, lanes] = part.T.astype(jnp.bfloat16)

    def table(c):
        lanes = lax.broadcasted_iota(jnp.int32, (CHUNK, 128), 1)
        unit = jnp.pi / NLON
        start, turn = [], []
        for w in range(WAVE):
            q = q_v[pl.ds(pl.multiple_of(w * SLOTS + c * CHUNK, 8), CHUNK), :]
            weight = jnp.where(q == 0.0, 1.0, 2.0)
            qi = q.astype(jnp.int32)
            first = lax.rem(qi * (2 * lanes + 1), 2 * NLON).astype(jnp.float32) * unit
            step = lax.rem(qi * 256, 2 * NLON).astype(jnp.float32) * unit
            start += [weight * jnp.cos(first), weight * jnp.sin(first)]
            turn += [jnp.cos(step), jnp.sin(step)]

        def tile(t, carry):
            carry = list(carry)
            for half in range(2):
                lon = slice(half * 128, (half + 1) * 128)
                for w in range(0, WAVE, 2):
                    rows = pl.ds(pl.multiple_of(c * 64 + w * 8, 16), 16)
                    for r in range(2):
                        t_ref[t, r, rows, lon] = jnp.concatenate(
                            [carry[2 * w + r], carry[2 * w + 2 + r]], axis=0
                        ).astype(jnp.bfloat16)
                for w in range(WAVE):
                    co, si = carry[2 * w], carry[2 * w + 1]
                    rc, rs = turn[2 * w], turn[2 * w + 1]
                    carry[2 * w] = co * rc - si * rs
                    carry[2 * w + 1] = si * rc + co * rs
            return tuple(carry)

        lax.fori_loop(0, LON_TILES, tile, tuple(start))

    leaf(0)
    for g in range(4):
        row = wm_ref[g : g + 1, :].astype(jnp.float32)
        q_v[g * 128 : (g + 1) * 128, :] = jnp.broadcast_to(row, (128, 128)).T
    phase = q_v[pl.ds(pl.multiple_of(me_w * SLOTS, 8), SLOTS), :] * (jnp.pi / NLON)
    ph_c[...] = jnp.cos(phase)
    ph_s[...] = jnp.sin(phase)
    pl.semaphore_wait(barrier, LEVELS + WAVE - 1)
    level_copy(0, 0).start()

    offsets = [0]
    for d in DELAY:
        offsets.append(offsets[-1] + d)

    def active(t, k):
        return jnp.logical_and(t >= offsets[k], t < offsets[k] + CHUNKS)

    def step(t, _):
        @pl.when(jnp.logical_and(t >= 1, t < CHUNKS))
        def _():
            leaf(t)
            level_copy(0, t).start()

        @pl.when(active(t, 1))
        def _():
            c = t - offsets[1]

            @pl.when(c == 0)
            def _():
                lev_load(0).wait()

            combine(0, c)
            level_copy(1, c).start()

        @pl.when(active(t, 2))
        def _():
            c = t - offsets[2]

            @pl.when(c == 0)
            def _():
                lev_load(1).wait()

            combine(1, c)
            level_copy(2, c).start()

        @pl.when(active(t, 3))
        def _():
            c = t - offsets[3]

            @pl.when(c == 0)
            def _():
                lev_load(2).wait()
                lat_load().wait()

            latitudes(c, combine(2, c))

        @pl.when(active(t, 4))
        def _():
            c = t - offsets[4]

            @pl.when(lax.rem(c, 2) == 1)
            def _():
                gathered(c // 2)

        @pl.when(t < CHUNKS)
        def _():
            table(t)

        return 0

    lax.fori_loop(0, CHUNKS + offsets[4], step, 0)

    def drain(c, _):
        for l in range(LEVELS):
            level_copy(l, c).wait_send()
        for d in range(1, WAVE):
            wave_copy(c, d).wait_send()
        return 0

    lax.fori_loop(0, CHUNKS, drain, 0)


def dft_kernel(xt_ref, t_ref, out_hbm, low, high, low_sem, high_sem):
    def copies(t, slot):
        near = pl.ds(pl.multiple_of(t * LON_TILE, LON_TILE), LON_TILE)
        far = pl.ds(pl.multiple_of((2 * LON_TILES - 1 - t) * LON_TILE, LON_TILE), LON_TILE)
        return (
            pltpu.make_async_copy(low.at[slot], out_hbm.at[:, near], low_sem.at[slot]),
            pltpu.make_async_copy(high.at[slot], out_hbm.at[:, far], high_sem.at[slot]),
        )

    mirror = 127 - lax.broadcasted_iota(jnp.int32, (512, 128), 1)

    def group(g, _):
        for k in range(UNROLL):
            t = g * UNROLL + k

            @pl.when(g > 0)
            def _():
                for copy in copies(t - UNROLL, k):
                    copy.wait()

        for k in range(UNROLL):
            t = g * UNROLL + k
            even = jnp.dot(xt_ref[0], t_ref[t, 0], preferred_element_type=jnp.float32)
            odd = jnp.dot(xt_ref[1], t_ref[t, 1], preferred_element_type=jnp.float32)
            low[k] = (even - odd).astype(jnp.bfloat16)
            total = even + odd
            for h in range(2):
                high[k, :, h * 128 : (h + 1) * 128] = jnp.take_along_axis(
                    total[:, (1 - h) * 128 : (2 - h) * 128], mirror, axis=1
                ).astype(jnp.bfloat16)
            for copy in copies(t, k):
                copy.start()
        return 0

    lax.fori_loop(0, LON_TILES // UNROLL, group, 0)
    for k in range(UNROLL):
        for copy in copies(LON_TILES - UNROLL + k, k):
            copy.wait()


def body(spectrum, leaf_map, level_maps, lat_map, skeleton, wavemap):
    any_spec = pl.BlockSpec(memory_space=pltpu.HBM)
    vmem_spec = pl.BlockSpec(memory_space=pltpu.VMEM)
    bf16, f32 = jnp.bfloat16, jnp.float32
    dma = pltpu.SemaphoreType.DMA
    xt, table = pl.pallas_call(
        comm_kernel,
        out_shape=(
            pltpu.VMEM((2, 512, 512), bf16),
            pltpu.VMEM((LON_TILES, 2, 512, LON_TILE), bf16),
        ),
        in_specs=[any_spec] * 4 + [vmem_spec] * 2,
        out_specs=(vmem_spec, vmem_spec),
        scratch_shapes=[
            pltpu.VMEM((SLOTS, COLS, 256), bf16),
            pltpu.VMEM((SLOTS, 256, NODE), bf16),
            pltpu.VMEM((LEVELS, SLOTS, NODE, NODE), bf16),
            pltpu.VMEM((SLOTS, NODE, NODE), bf16),
            pltpu.VMEM((SLOTS, COLS, NODE), bf16),
            pltpu.VMEM((LEVELS, SLOTS // 2, COLS, NODE), bf16),
            pltpu.VMEM((LEVELS, SLOTS // 2, COLS, NODE), bf16),
            pltpu.VMEM((CHUNK * COLS, NODE), f32),
            pltpu.VMEM((CHUNKS, WAVE, 64, NODE), bf16),
            pltpu.VMEM((CHUNKS, WAVE, 64, NODE), bf16),
            pltpu.VMEM((512, 128), f32),
            pltpu.VMEM((SLOTS, 128), f32),
            pltpu.VMEM((SLOTS, 128), f32),
            dma((CHUNKS,)),
            dma((CHUNKS,)),
            dma((LEVELS,)),
            dma((1,)),
            dma((LEVELS, CHUNKS)),
            dma((LEVELS, CHUNKS)),
            dma((CHUNKS, WAVE - 1)),
            dma((CHUNKS, WAVE - 1)),
        ],
        compiler_params=pltpu.CompilerParams(
            collective_id=0, has_side_effects=True, vmem_limit_bytes=VMEM_FIRST * 1024 * 1024
        ),
    )(
        spectrum.reshape(SLOTS, COLS, 256),
        leaf_map,
        level_maps,
        lat_map,
        skeleton,
        wavemap.reshape(4, 128),
    )
    grid = pl.pallas_call(
        dft_kernel,
        out_shape=jax.ShapeDtypeStruct((512, NLON), bf16),
        in_specs=[vmem_spec, vmem_spec],
        out_specs=any_spec,
        scratch_shapes=[
            pltpu.VMEM((UNROLL, 512, LON_TILE), bf16),
            pltpu.VMEM((UNROLL, 512, LON_TILE), bf16),
            dma((UNROLL,)),
            dma((UNROLL,)),
        ],
        compiler_params=pltpu.CompilerParams(vmem_limit_bytes=VMEM_SECOND * 1024 * 1024),
    )(xt, table)
    return grid.reshape(4, 128, NLON)


def solution(mesh):
    placed = (
        P("wave", None, None, "deg"),
        P("wave", "deg", None),
        P(None, "wave", "deg", None),
        P("wave", None, "deg"),
        P("wave", "deg"),
        P(),
    )
    return jax.shard_map(
        body, mesh=mesh, in_specs=placed, out_specs=P("wave", "deg", None), check_vma=False
    )
```

```python
import jax
import jax.numpy as jnp
from jax import lax
from jax.experimental import pallas as pl
from jax.experimental.pallas import tpu as pltpu
from jax.sharding import PartitionSpec as P

NLON = 8192
LEVELS = 3
SLOTS = 64
CHUNK = 8
CHUNKS = SLOTS // CHUNK
PAIRS = CHUNK // 2
COLS = 64
NODE = 128
WAVE = 8
LON_TILE = 256
LON_TILES = NLON // 2 // LON_TILE
MESH = pl.DeviceIdType.MESH
DELAY = (3, 3, 2, 3)
UNROLL = 4
VMEM_FIRST = 37
VMEM_SECOND = 16


def comm_kernel(
    spec_hbm, leaf_hbm, lev_hbm, lat_hbm, skel_ref, wm_ref,
    xt_ref, t_ref, part_ref,
    spec_v, leaf_v, lev_v, lat_v, state, send, recv, lat32, a_send, a_recv, q_v, ph_c, ph_s,
    spec_sem, leaf_sem, lev_sem, lat_sem, l_ssem, l_rsem, a_ssem, a_rsem,
):
    me_w = lax.axis_index("wave")
    me_d = lax.axis_index("deg")
    lane_half = lax.broadcasted_iota(jnp.int32, (COLS, NODE), 1) // (NODE // 2)

    def spec_load(c):
        rows = pl.ds(c * CHUNK, CHUNK)
        return pltpu.make_async_copy(spec_hbm.at[rows], spec_v.at[rows], spec_sem.at[c])

    def leaf_load(c):
        rows = pl.ds(c * CHUNK, CHUNK)
        return pltpu.make_async_copy(leaf_hbm.at[rows], leaf_v.at[rows], leaf_sem.at[c])

    def lev_load(l):
        return pltpu.make_async_copy(lev_hbm.at[l], lev_v.at[l], lev_sem.at[l])

    def lat_load():
        return pltpu.make_async_copy(lat_hbm, lat_v, lat_sem.at[0])

    def level_copy(l, c):
        rows = pl.ds(c * PAIRS, PAIRS)
        return pltpu.make_async_remote_copy(
            src_ref=send.at[l, rows],
            dst_ref=recv.at[l, rows],
            send_sem=l_ssem.at[l, c],
            recv_sem=l_rsem.at[l, c],
            device_id={"deg": me_d ^ (1 << l)},
            device_id_type=MESH,
        )

    def wave_copy(c, d, arriving=False):
        target = lax.rem(me_w + d, WAVE)
        place = lax.rem(me_w + WAVE - d, WAVE) if arriving else me_w
        return pltpu.make_async_remote_copy(
            src_ref=a_send.at[c, target],
            dst_ref=a_recv.at[c, place],
            send_sem=a_ssem.at[c, d - 1],
            recv_sem=a_rsem.at[c, d - 1],
            device_id={"wave": target},
            device_id_type=MESH,
        )

    for c in range(CHUNKS):
        spec_load(c).start()
        leaf_load(c).start()
    for l in range(LEVELS):
        lev_load(l).start()
    lat_load().start()

    barrier = pltpu.get_barrier_semaphore()
    for l in range(LEVELS):
        pl.semaphore_signal(barrier, inc=1, device_id={"deg": me_d ^ (1 << l)}, device_id_type=MESH)
    for d in range(1, WAVE):
        pl.semaphore_signal(
            barrier, inc=1, device_id={"wave": lax.rem(me_w + d, WAVE)}, device_id_type=MESH
        )

    def pack(l, c, values):
        s = lax.rem(me_d // (1 << l), 2)
        mask = lane_half == 1 - s
        upper = jnp.broadcast_to(s, (COLS, NODE)) == 1
        for p in range(PAIRS):
            even, odd = values[2 * p], values[2 * p + 1]
            kept = jnp.where(upper, even, odd)
            moved = pltpu.roll(jnp.where(upper, odd, even), NODE // 2, 1)
            send[l, c * PAIRS + p] = jnp.where(mask, kept, moved)

    def leaf(c):
        spec_load(c).wait()
        leaf_load(c).wait()
        degree = lax.broadcasted_iota(jnp.int32, (256, NODE), 0)
        values = []
        for j in range(CHUNK):
            m = c * CHUNK + j
            coef = spec_v[m]
            picks = jnp.where(degree == skel_ref[pl.ds(m, 1), :], 1.0, 0.0).astype(jnp.bfloat16)
            acc = jnp.dot(coef, picks, preferred_element_type=jnp.float32)
            acc = acc + jnp.dot(coef, leaf_v[m], preferred_element_type=jnp.float32)
            values.append(acc.astype(jnp.bfloat16))
        for j in range(CHUNK):
            state[c * CHUNK + j] = values[j]
        pack(0, c, values)

    def combine(l, c):
        level_copy(l, c).wait_recv()
        s = lax.rem(me_d // (1 << l), 2)
        mask = lane_half == s
        upper = jnp.broadcast_to(s, (COLS, NODE)) == 1
        joined = []
        for p in range(PAIRS):
            got = recv[l, c * PAIRS + p]
            turned = pltpu.roll(got, NODE // 2, 1)
            for j, other in (
                (2 * p, jnp.where(upper, got, turned)),
                (2 * p + 1, jnp.where(upper, turned, got)),
            ):
                joined.append(jnp.where(mask, state[c * CHUNK + j], other))
        values = [
            jnp.dot(joined[j], lev_v[l, c * CHUNK + j], preferred_element_type=jnp.float32).astype(
                jnp.bfloat16
            )
            for j in range(CHUNK)
        ]
        if l < LEVELS - 1:
            for j in range(CHUNK):
                state[c * CHUNK + j] = values[j]
            pack(l + 1, c, values)
        return values

    def latitudes(c, values):
        for j in range(CHUNK):
            rows = jnp.dot(values[j], lat_v[c * CHUNK + j], preferred_element_type=jnp.float32)
            real, imag = rows[:32], rows[32:]
            at = pl.ds(c * CHUNK + j, 1)
            co, si = ph_c[at, :], ph_s[at, :]
            lat32[pl.ds(j, 32, stride=2 * CHUNK), :] = real * co + imag * si
            lat32[pl.ds(CHUNK + j, 32, stride=2 * CHUNK), :] = imag * co - real * si
        for w in range(WAVE):
            a_send[c, w] = lat32[w * 64 : (w + 1) * 64, :].astype(jnp.bfloat16)
        a_recv[c, me_w] = a_send[c, me_w]
        for d in (4, 3, 5, 2, 6, 1, 7):
            wave_copy(c, d).start()

    def gathered(pair):
        for k in range(2):
            for d in range(1, WAVE):
                wave_copy(2 * pair + k, d, True).wait_recv()
        lanes = pl.ds(pl.multiple_of(pair * 128, 128), 128)
        for f in range(4):
            block = jnp.concatenate(
                [
                    a_recv[2 * pair + k, :, f * 16 : (f + 1) * 16, :].astype(jnp.float32)
                    for k in range(2)
                ],
                axis=0,
            )
            for r in range(2):
                part = block[:, r * 8 : (r + 1) * 8, :].reshape(128, 128)
                xt_ref[r, f * 128 : (f + 1) * 128, lanes] = part.T.astype(jnp.bfloat16)

    def table(c):
        lanes = lax.broadcasted_iota(jnp.int32, (CHUNK, 128), 1)
        unit = jnp.pi / NLON
        start, turn = [], []
        for w in range(WAVE):
            q = q_v[pl.ds(pl.multiple_of(w * SLOTS + c * CHUNK, 8), CHUNK), :]
            weight = jnp.where(q == 0.0, 1.0, 2.0)
            qi = q.astype(jnp.int32)
            first = lax.rem(qi * (2 * lanes + 1), 2 * NLON).astype(jnp.float32) * unit
            step = lax.rem(qi * 256, 2 * NLON).astype(jnp.float32) * unit
            start += [weight * jnp.cos(first), weight * jnp.sin(first)]
            turn += [jnp.cos(step), jnp.sin(step)]

        def tile(t, carry):
            carry = list(carry)
            for half in range(2):
                lon = slice(half * 128, (half + 1) * 128)
                for w in range(0, WAVE, 2):
                    rows = pl.ds(pl.multiple_of(c * 64 + w * 8, 16), 16)
                    for r in range(2):
                        t_ref[t, r, rows, lon] = jnp.concatenate(
                            [carry[2 * w + r], carry[2 * w + 2 + r]], axis=0
                        ).astype(jnp.bfloat16)
                for w in range(WAVE):
                    co, si = carry[2 * w], carry[2 * w + 1]
                    rc, rs = turn[2 * w], turn[2 * w + 1]
                    carry[2 * w] = co * rc - si * rs
                    carry[2 * w + 1] = si * rc + co * rs
            return tuple(carry)

        lax.fori_loop(0, LON_TILES, tile, tuple(start))

    def early(at):
        def group(g, _):
            for k in range(UNROLL):
                t = at + g * UNROLL + k
                for r in range(2):
                    part_ref[t, r] = jnp.dot(
                        xt_ref[r, :, :256], t_ref[t, r, :256], preferred_element_type=jnp.float32
                    )
            return 0

        lax.fori_loop(0, LON_TILES // 2 // UNROLL, group, 0)

    leaf(0)
    for g in range(4):
        row = wm_ref[g : g + 1, :].astype(jnp.float32)
        q_v[g * 128 : (g + 1) * 128, :] = jnp.broadcast_to(row, (128, 128)).T
    phase = q_v[pl.ds(pl.multiple_of(me_w * SLOTS, 8), SLOTS), :] * (jnp.pi / NLON)
    ph_c[...] = jnp.cos(phase)
    ph_s[...] = jnp.sin(phase)
    pl.semaphore_wait(barrier, LEVELS + WAVE - 1)
    level_copy(0, 0).start()

    offsets = [0]
    for d in DELAY:
        offsets.append(offsets[-1] + d)

    def active(t, k):
        return jnp.logical_and(t >= offsets[k], t < offsets[k] + CHUNKS)

    def step(t, _):
        @pl.when(jnp.logical_and(t >= 1, t < CHUNKS))
        def _():
            leaf(t)
            level_copy(0, t).start()

        @pl.when(active(t, 1))
        def _():
            c = t - offsets[1]

            @pl.when(c == 0)
            def _():
                lev_load(0).wait()

            combine(0, c)
            level_copy(1, c).start()

        @pl.when(active(t, 2))
        def _():
            c = t - offsets[2]

            @pl.when(c == 0)
            def _():
                lev_load(1).wait()

            combine(1, c)
            level_copy(2, c).start()

        @pl.when(active(t, 3))
        def _():
            c = t - offsets[3]

            @pl.when(c == 0)
            def _():
                lev_load(2).wait()
                lat_load().wait()

            latitudes(c, combine(2, c))

        @pl.when(active(t, 4))
        def _():
            c = t - offsets[4]

            @pl.when(lax.rem(c, 2) == 1)
            def _():
                gathered(c // 2)

        @pl.when(t < CHUNKS)
        def _():
            table(t)

        @pl.when(t == offsets[3] + CHUNKS - 1)
        def _():
            early(0)
            early(LON_TILES // 2)

        return 0

    lax.fori_loop(0, CHUNKS + offsets[4], step, 0)

    def drain(c, _):
        for l in range(LEVELS):
            level_copy(l, c).wait_send()
        for d in range(1, WAVE):
            wave_copy(c, d).wait_send()
        return 0

    lax.fori_loop(0, CHUNKS, drain, 0)


def dft_kernel(xt_ref, t_ref, part_ref, out_hbm, low, high, low_sem, high_sem):
    def copies(t, slot):
        near = pl.ds(pl.multiple_of(t * LON_TILE, LON_TILE), LON_TILE)
        far = pl.ds(pl.multiple_of((2 * LON_TILES - 1 - t) * LON_TILE, LON_TILE), LON_TILE)
        return (
            pltpu.make_async_copy(low.at[slot], out_hbm.at[:, near], low_sem.at[slot]),
            pltpu.make_async_copy(high.at[slot], out_hbm.at[:, far], high_sem.at[slot]),
        )

    mirror = 127 - lax.broadcasted_iota(jnp.int32, (512, 128), 1)

    def group(g, _):
        for k in range(UNROLL):
            t = g * UNROLL + k

            @pl.when(g > 0)
            def _():
                for copy in copies(t - UNROLL, k):
                    copy.wait()

        for k in range(UNROLL):
            t = g * UNROLL + k
            even, odd = (
                part_ref[t, r]
                + jnp.dot(
                    xt_ref[r, :, 256:], t_ref[t, r, 256:], preferred_element_type=jnp.float32
                )
                for r in range(2)
            )
            low[k] = (even - odd).astype(jnp.bfloat16)
            total = even + odd
            for h in range(2):
                high[k, :, h * 128 : (h + 1) * 128] = jnp.take_along_axis(
                    total[:, (1 - h) * 128 : (2 - h) * 128], mirror, axis=1
                ).astype(jnp.bfloat16)
            for copy in copies(t, k):
                copy.start()
        return 0

    lax.fori_loop(0, LON_TILES // UNROLL, group, 0)
    for k in range(UNROLL):
        for copy in copies(LON_TILES - UNROLL + k, k):
            copy.wait()


def body(spectrum, leaf_map, level_maps, lat_map, skeleton, wavemap):
    any_spec = pl.BlockSpec(memory_space=pltpu.HBM)
    vmem_spec = pl.BlockSpec(memory_space=pltpu.VMEM)
    bf16, f32 = jnp.bfloat16, jnp.float32
    dma = pltpu.SemaphoreType.DMA
    xt, table, part = pl.pallas_call(
        comm_kernel,
        out_shape=(
            pltpu.VMEM((2, 512, 512), bf16),
            pltpu.VMEM((LON_TILES, 2, 512, LON_TILE), bf16),
            pltpu.VMEM((LON_TILES, 2, 512, LON_TILE), f32),
        ),
        in_specs=[any_spec] * 4 + [vmem_spec] * 2,
        out_specs=(vmem_spec,) * 3,
        scratch_shapes=[
            pltpu.VMEM((SLOTS, COLS, 256), bf16),
            pltpu.VMEM((SLOTS, 256, NODE), bf16),
            pltpu.VMEM((LEVELS, SLOTS, NODE, NODE), bf16),
            pltpu.VMEM((SLOTS, NODE, NODE), bf16),
            pltpu.VMEM((SLOTS, COLS, NODE), bf16),
            pltpu.VMEM((LEVELS, SLOTS // 2, COLS, NODE), bf16),
            pltpu.VMEM((LEVELS, SLOTS // 2, COLS, NODE), bf16),
            pltpu.VMEM((CHUNK * COLS, NODE), f32),
            pltpu.VMEM((CHUNKS, WAVE, 64, NODE), bf16),
            pltpu.VMEM((CHUNKS, WAVE, 64, NODE), bf16),
            pltpu.VMEM((512, 128), f32),
            pltpu.VMEM((SLOTS, 128), f32),
            pltpu.VMEM((SLOTS, 128), f32),
            dma((CHUNKS,)),
            dma((CHUNKS,)),
            dma((LEVELS,)),
            dma((1,)),
            dma((LEVELS, CHUNKS)),
            dma((LEVELS, CHUNKS)),
            dma((CHUNKS, WAVE - 1)),
            dma((CHUNKS, WAVE - 1)),
        ],
        compiler_params=pltpu.CompilerParams(
            collective_id=0, has_side_effects=True, vmem_limit_bytes=VMEM_FIRST * 1024 * 1024
        ),
    )(
        spectrum.reshape(SLOTS, COLS, 256),
        leaf_map,
        level_maps,
        lat_map,
        skeleton,
        wavemap.reshape(4, 128),
    )
    grid = pl.pallas_call(
        dft_kernel,
        out_shape=jax.ShapeDtypeStruct((512, NLON), bf16),
        in_specs=[vmem_spec] * 3,
        out_specs=any_spec,
        scratch_shapes=[
            pltpu.VMEM((UNROLL, 512, LON_TILE), bf16),
            pltpu.VMEM((UNROLL, 512, LON_TILE), bf16),
            dma((UNROLL,)),
            dma((UNROLL,)),
        ],
        compiler_params=pltpu.CompilerParams(vmem_limit_bytes=VMEM_SECOND * 1024 * 1024),
    )(xt, table, part)
    return grid.reshape(4, 128, NLON)


def solution(mesh):
    placed = (
        P("wave", None, None, "deg"),
        P("wave", "deg", None),
        P(None, "wave", "deg", None),
        P("wave", None, "deg"),
        P("wave", "deg"),
        P(),
    )
    return jax.shard_map(
        body, mesh=mesh, in_specs=placed, out_specs=P("wave", "deg", None), check_vma=False
    )
```

```python
import jax
import jax.numpy as jnp
from jax import lax
from jax.experimental import pallas as pl
from jax.experimental.pallas import tpu as pltpu
from jax.sharding import PartitionSpec as P

NLON = 8192
LEVELS = 3
SLOTS = 64
CHUNK = 8
CHUNKS = SLOTS // CHUNK
PAIRS = CHUNK // 2
COLS = 64
NODE = 128
WAVE = 8
LON_TILE = 256
LON_TILES = NLON // 2 // LON_TILE
MESH = pl.DeviceIdType.MESH
DELAY = (3, 3, 2, 3)
UNROLL = 16
EARLY = 4
VMEM_FIRST = 37
VMEM_SECOND = 16


def comm_kernel(
    spec_hbm, leaf_hbm, lev_hbm, lat_hbm, skel_ref, wm_ref,
    xt_ref, t_ref, part_ref,
    spec_v, leaf_v, lev_v, lat_v, state, send, recv, lat32, a_send, a_recv, q_v, ph_c, ph_s,
    spec_sem, leaf_sem, lev_sem, lat_sem, l_ssem, l_rsem, a_ssem, a_rsem,
):
    me_w = lax.axis_index("wave")
    me_d = lax.axis_index("deg")
    lane_half = lax.broadcasted_iota(jnp.int32, (COLS, NODE), 1) // (NODE // 2)

    def spec_load(c):
        rows = pl.ds(c * CHUNK, CHUNK)
        return pltpu.make_async_copy(spec_hbm.at[rows], spec_v.at[rows], spec_sem.at[c])

    def leaf_load(c):
        rows = pl.ds(c * CHUNK, CHUNK)
        return pltpu.make_async_copy(leaf_hbm.at[rows], leaf_v.at[rows], leaf_sem.at[c])

    def lev_load(l):
        return pltpu.make_async_copy(lev_hbm.at[l], lev_v.at[l], lev_sem.at[l])

    def lat_load():
        return pltpu.make_async_copy(lat_hbm, lat_v, lat_sem.at[0])

    def level_copy(l, c):
        rows = pl.ds(c * PAIRS, PAIRS)
        return pltpu.make_async_remote_copy(
            src_ref=send.at[l, rows],
            dst_ref=recv.at[l, rows],
            send_sem=l_ssem.at[l, c],
            recv_sem=l_rsem.at[l, c],
            device_id={"deg": me_d ^ (1 << l)},
            device_id_type=MESH,
        )

    def wave_copy(c, d, arriving=False):
        target = lax.rem(me_w + d, WAVE)
        place = lax.rem(me_w + WAVE - d, WAVE) if arriving else me_w
        return pltpu.make_async_remote_copy(
            src_ref=a_send.at[c, target],
            dst_ref=a_recv.at[c, place],
            send_sem=a_ssem.at[c, d - 1],
            recv_sem=a_rsem.at[c, d - 1],
            device_id={"wave": target},
            device_id_type=MESH,
        )

    for c in range(CHUNKS):
        spec_load(c).start()
        leaf_load(c).start()
    for l in range(LEVELS):
        lev_load(l).start()
    lat_load().start()

    barrier = pltpu.get_barrier_semaphore()
    for l in range(LEVELS):
        pl.semaphore_signal(barrier, inc=1, device_id={"deg": me_d ^ (1 << l)}, device_id_type=MESH)
    for d in range(1, WAVE):
        pl.semaphore_signal(
            barrier, inc=1, device_id={"wave": lax.rem(me_w + d, WAVE)}, device_id_type=MESH
        )

    def pack(l, c, values):
        s = lax.rem(me_d // (1 << l), 2)
        mask = lane_half == 1 - s
        upper = jnp.broadcast_to(s, (COLS, NODE)) == 1
        for p in range(PAIRS):
            even, odd = values[2 * p], values[2 * p + 1]
            kept = jnp.where(upper, even, odd)
            moved = pltpu.roll(jnp.where(upper, odd, even), NODE // 2, 1)
            send[l, c * PAIRS + p] = jnp.where(mask, kept, moved)

    def leaf(c):
        spec_load(c).wait()
        leaf_load(c).wait()
        degree = lax.broadcasted_iota(jnp.int32, (256, NODE), 0)
        values = []
        for j in range(CHUNK):
            m = c * CHUNK + j
            coef = spec_v[m]
            picks = jnp.where(degree == skel_ref[pl.ds(m, 1), :], 1.0, 0.0).astype(jnp.bfloat16)
            acc = jnp.dot(coef, picks, preferred_element_type=jnp.float32)
            acc = acc + jnp.dot(coef, leaf_v[m], preferred_element_type=jnp.float32)
            values.append(acc.astype(jnp.bfloat16))
        for j in range(CHUNK):
            state[c * CHUNK + j] = values[j]
        pack(0, c, values)

    def combine(l, c):
        level_copy(l, c).wait_recv()
        s = lax.rem(me_d // (1 << l), 2)
        mask = lane_half == s
        upper = jnp.broadcast_to(s, (COLS, NODE)) == 1
        joined = []
        for p in range(PAIRS):
            got = recv[l, c * PAIRS + p]
            turned = pltpu.roll(got, NODE // 2, 1)
            for j, other in (
                (2 * p, jnp.where(upper, got, turned)),
                (2 * p + 1, jnp.where(upper, turned, got)),
            ):
                joined.append(jnp.where(mask, state[c * CHUNK + j], other))
        values = [
            jnp.dot(joined[j], lev_v[l, c * CHUNK + j], preferred_element_type=jnp.float32).astype(
                jnp.bfloat16
            )
            for j in range(CHUNK)
        ]
        if l < LEVELS - 1:
            for j in range(CHUNK):
                state[c * CHUNK + j] = values[j]
            pack(l + 1, c, values)
        return values

    def latitudes(c, values):
        for j in range(CHUNK):
            rows = jnp.dot(values[j], lat_v[c * CHUNK + j], preferred_element_type=jnp.float32)
            real, imag = rows[:32], rows[32:]
            at = pl.ds(c * CHUNK + j, 1)
            co, si = ph_c[at, :], ph_s[at, :]
            lat32[pl.ds(j, 32, stride=2 * CHUNK), :] = real * co + imag * si
            lat32[pl.ds(CHUNK + j, 32, stride=2 * CHUNK), :] = imag * co - real * si
        for w in range(WAVE):
            a_send[c, w] = lat32[w * 64 : (w + 1) * 64, :].astype(jnp.bfloat16)
        a_recv[c, me_w] = a_send[c, me_w]
        for d in (4, 3, 5, 2, 6, 1, 7):
            wave_copy(c, d).start()

    def gathered(pair):
        for k in range(2):
            for d in range(1, WAVE):
                wave_copy(2 * pair + k, d, True).wait_recv()
        lanes = pl.ds(pl.multiple_of(pair * 128, 128), 128)
        for f in range(4):
            block = jnp.concatenate(
                [
                    a_recv[2 * pair + k, :, f * 16 : (f + 1) * 16, :].astype(jnp.float32)
                    for k in range(2)
                ],
                axis=0,
            )
            for r in range(2):
                part = block[:, r * 8 : (r + 1) * 8, :].reshape(128, 128)
                xt_ref[r, f * 128 : (f + 1) * 128, lanes] = part.T.astype(jnp.bfloat16)

    def table(c):
        lanes = lax.broadcasted_iota(jnp.int32, (CHUNK, 128), 1)
        unit = jnp.pi / NLON
        start, turn = [], []
        for w in range(WAVE):
            q = q_v[pl.ds(pl.multiple_of(w * SLOTS + c * CHUNK, 8), CHUNK), :]
            weight = jnp.where(q == 0.0, 1.0, 2.0)
            qi = q.astype(jnp.int32)
            first = lax.rem(qi * (2 * lanes + 1), 2 * NLON).astype(jnp.float32) * unit
            step = lax.rem(qi * 256, 2 * NLON).astype(jnp.float32) * unit
            start += [weight * jnp.cos(first), weight * jnp.sin(first)]
            turn += [jnp.cos(step), jnp.sin(step)]

        def tile(t, carry):
            carry = list(carry)
            for half in range(2):
                lon = slice(half * 128, (half + 1) * 128)
                for w in range(0, WAVE, 2):
                    rows = pl.ds(pl.multiple_of(c * 64 + w * 8, 16), 16)
                    for r in range(2):
                        t_ref[t, r, rows, lon] = jnp.concatenate(
                            [carry[2 * w + r], carry[2 * w + 2 + r]], axis=0
                        ).astype(jnp.bfloat16)
                for w in range(WAVE):
                    co, si = carry[2 * w], carry[2 * w + 1]
                    rc, rs = turn[2 * w], turn[2 * w + 1]
                    carry[2 * w] = co * rc - si * rs
                    carry[2 * w + 1] = si * rc + co * rs
            return tuple(carry)

        lax.fori_loop(0, LON_TILES, tile, tuple(start))

    def early(at):
        def group(g, _):
            for k in range(EARLY):
                t = at + g * EARLY + k
                for r in range(2):
                    part_ref[t, r] = jnp.dot(
                        xt_ref[r, :, :256], t_ref[t, r, :256], preferred_element_type=jnp.float32
                    )
            return 0

        lax.fori_loop(0, LON_TILES // 2 // EARLY, group, 0)

    leaf(0)
    for g in range(4):
        row = wm_ref[g : g + 1, :].astype(jnp.float32)
        q_v[g * 128 : (g + 1) * 128, :] = jnp.broadcast_to(row, (128, 128)).T
    phase = q_v[pl.ds(pl.multiple_of(me_w * SLOTS, 8), SLOTS), :] * (jnp.pi / NLON)
    ph_c[...] = jnp.cos(phase)
    ph_s[...] = jnp.sin(phase)
    pl.semaphore_wait(barrier, LEVELS + WAVE - 1)
    level_copy(0, 0).start()

    offsets = [0]
    for d in DELAY:
        offsets.append(offsets[-1] + d)

    def active(t, k):
        return jnp.logical_and(t >= offsets[k], t < offsets[k] + CHUNKS)

    def step(t, _):
        @pl.when(jnp.logical_and(t >= 1, t < CHUNKS))
        def _():
            leaf(t)
            level_copy(0, t).start()

        @pl.when(active(t, 1))
        def _():
            c = t - offsets[1]

            @pl.when(c == 0)
            def _():
                lev_load(0).wait()

            combine(0, c)
            level_copy(1, c).start()

        @pl.when(active(t, 2))
        def _():
            c = t - offsets[2]

            @pl.when(c == 0)
            def _():
                lev_load(1).wait()

            combine(1, c)
            level_copy(2, c).start()

        @pl.when(active(t, 3))
        def _():
            c = t - offsets[3]

            @pl.when(c == 0)
            def _():
                lev_load(2).wait()
                lat_load().wait()

            latitudes(c, combine(2, c))

        @pl.when(active(t, 4))
        def _():
            c = t - offsets[4]

            @pl.when(lax.rem(c, 2) == 1)
            def _():
                gathered(c // 2)

        @pl.when(t < CHUNKS)
        def _():
            table(t)

        @pl.when(t == offsets[3] + CHUNKS - 1)
        def _():
            early(0)
            early(LON_TILES // 2)

        return 0

    lax.fori_loop(0, CHUNKS + offsets[4], step, 0)

    def drain(c, _):
        for l in range(LEVELS):
            level_copy(l, c).wait_send()
        for d in range(1, WAVE):
            wave_copy(c, d).wait_send()
        return 0

    lax.fori_loop(0, CHUNKS, drain, 0)


def dft_kernel(xt_ref, t_ref, part_ref, out_hbm, low, high, low_sem, high_sem):
    def copies(t, slot):
        near = pl.ds(pl.multiple_of(t * LON_TILE, LON_TILE), LON_TILE)
        far = pl.ds(pl.multiple_of((2 * LON_TILES - 1 - t) * LON_TILE, LON_TILE), LON_TILE)
        return (
            pltpu.make_async_copy(low.at[slot], out_hbm.at[:, near], low_sem.at[slot]),
            pltpu.make_async_copy(high.at[slot], out_hbm.at[:, far], high_sem.at[slot]),
        )

    mirror = 127 - lax.broadcasted_iota(jnp.int32, (512, 128), 1)

    def group(g, _):
        for k in range(UNROLL):
            t = g * UNROLL + k

            @pl.when(g > 0)
            def _():
                for copy in copies(t - UNROLL, k):
                    copy.wait()

        for k in range(UNROLL):
            t = g * UNROLL + k
            even, odd = (
                part_ref[t, r]
                + jnp.dot(
                    xt_ref[r, :, 256:], t_ref[t, r, 256:], preferred_element_type=jnp.float32
                )
                for r in range(2)
            )
            low[k] = (even - odd).astype(jnp.bfloat16)
            total = even + odd
            for h in range(2):
                high[k, :, h * 128 : (h + 1) * 128] = jnp.take_along_axis(
                    total[:, (1 - h) * 128 : (2 - h) * 128], mirror, axis=1
                ).astype(jnp.bfloat16)
            for copy in copies(t, k):
                copy.start()
        return 0

    lax.fori_loop(0, LON_TILES // UNROLL, group, 0)
    for k in range(UNROLL):
        for copy in copies(LON_TILES - UNROLL + k, k):
            copy.wait()


def body(spectrum, leaf_map, level_maps, lat_map, skeleton, wavemap):
    any_spec = pl.BlockSpec(memory_space=pltpu.HBM)
    vmem_spec = pl.BlockSpec(memory_space=pltpu.VMEM)
    bf16, f32 = jnp.bfloat16, jnp.float32
    dma = pltpu.SemaphoreType.DMA
    xt, table, part = pl.pallas_call(
        comm_kernel,
        out_shape=(
            pltpu.VMEM((2, 512, 512), bf16),
            pltpu.VMEM((LON_TILES, 2, 512, LON_TILE), bf16),
            pltpu.VMEM((LON_TILES, 2, 512, LON_TILE), f32),
        ),
        in_specs=[any_spec] * 4 + [vmem_spec] * 2,
        out_specs=(vmem_spec,) * 3,
        scratch_shapes=[
            pltpu.VMEM((SLOTS, COLS, 256), bf16),
            pltpu.VMEM((SLOTS, 256, NODE), bf16),
            pltpu.VMEM((LEVELS, SLOTS, NODE, NODE), bf16),
            pltpu.VMEM((SLOTS, NODE, NODE), bf16),
            pltpu.VMEM((SLOTS, COLS, NODE), bf16),
            pltpu.VMEM((LEVELS, SLOTS // 2, COLS, NODE), bf16),
            pltpu.VMEM((LEVELS, SLOTS // 2, COLS, NODE), bf16),
            pltpu.VMEM((CHUNK * COLS, NODE), f32),
            pltpu.VMEM((CHUNKS, WAVE, 64, NODE), bf16),
            pltpu.VMEM((CHUNKS, WAVE, 64, NODE), bf16),
            pltpu.VMEM((512, 128), f32),
            pltpu.VMEM((SLOTS, 128), f32),
            pltpu.VMEM((SLOTS, 128), f32),
            dma((CHUNKS,)),
            dma((CHUNKS,)),
            dma((LEVELS,)),
            dma((1,)),
            dma((LEVELS, CHUNKS)),
            dma((LEVELS, CHUNKS)),
            dma((CHUNKS, WAVE - 1)),
            dma((CHUNKS, WAVE - 1)),
        ],
        compiler_params=pltpu.CompilerParams(
            collective_id=0, has_side_effects=True, vmem_limit_bytes=VMEM_FIRST * 1024 * 1024
        ),
    )(
        spectrum.reshape(SLOTS, COLS, 256),
        leaf_map,
        level_maps,
        lat_map,
        skeleton,
        wavemap.reshape(4, 128),
    )
    grid = pl.pallas_call(
        dft_kernel,
        out_shape=jax.ShapeDtypeStruct((512, NLON), bf16),
        in_specs=[vmem_spec] * 3,
        out_specs=any_spec,
        scratch_shapes=[
            pltpu.VMEM((UNROLL, 512, LON_TILE), bf16),
            pltpu.VMEM((UNROLL, 512, LON_TILE), bf16),
            dma((UNROLL,)),
            dma((UNROLL,)),
        ],
        compiler_params=pltpu.CompilerParams(vmem_limit_bytes=VMEM_SECOND * 1024 * 1024),
    )(xt, table, part)
    return grid.reshape(4, 128, NLON)


def solution(mesh):
    placed = (
        P("wave", None, None, "deg"),
        P("wave", "deg", None),
        P(None, "wave", "deg", None),
        P("wave", None, "deg"),
        P("wave", "deg"),
        P(),
    )
    return jax.shard_map(
        body, mesh=mesh, in_specs=placed, out_specs=P("wave", "deg", None), check_vma=False
    )
```

```python
import jax
import jax.numpy as jnp
from jax import lax
from jax.experimental import pallas as pl
from jax.experimental.pallas import tpu as pltpu
from jax.sharding import PartitionSpec as P

NLON = 8192
LEVELS = 3
SLOTS = 64
CHUNK = 8
CHUNKS = SLOTS // CHUNK
PAIRS = CHUNK // 2
COLS = 64
NODE = 128
WAVE = 8
LON_TILE = 256
LON_TILES = NLON // 2 // LON_TILE
MESH = pl.DeviceIdType.MESH
DELAY = (2, 3, 2, 3)
UNROLL = 16
EARLY = 4
VMEM_FIRST = 37
VMEM_SECOND = 16


def comm_kernel(
    spec_hbm, leaf_hbm, lev_hbm, lat_hbm, skel_ref, wm_ref,
    xt_ref, t_ref, part_ref,
    spec_v, leaf_v, lev_v, lat_v, state, send, recv, lat32, a_send, a_recv, q_v, ph_c, ph_s,
    spec_sem, leaf_sem, lev_sem, lat_sem, l_ssem, l_rsem, a_ssem, a_rsem,
):
    me_w = lax.axis_index("wave")
    me_d = lax.axis_index("deg")
    lane_half = lax.broadcasted_iota(jnp.int32, (COLS, NODE), 1) // (NODE // 2)

    def spec_load(c):
        rows = pl.ds(c * CHUNK, CHUNK)
        return pltpu.make_async_copy(spec_hbm.at[rows], spec_v.at[rows], spec_sem.at[c])

    def leaf_load(c):
        rows = pl.ds(c * CHUNK, CHUNK)
        return pltpu.make_async_copy(leaf_hbm.at[rows], leaf_v.at[rows], leaf_sem.at[c])

    def lev_load(l):
        return pltpu.make_async_copy(lev_hbm.at[l], lev_v.at[l], lev_sem.at[l])

    def lat_load():
        return pltpu.make_async_copy(lat_hbm, lat_v, lat_sem.at[0])

    def level_copy(l, c):
        rows = pl.ds(c * PAIRS, PAIRS)
        return pltpu.make_async_remote_copy(
            src_ref=send.at[l, rows],
            dst_ref=recv.at[l, rows],
            send_sem=l_ssem.at[l, c],
            recv_sem=l_rsem.at[l, c],
            device_id={"deg": me_d ^ (1 << l)},
            device_id_type=MESH,
        )

    def wave_copy(c, d, arriving=False):
        target = lax.rem(me_w + d, WAVE)
        place = lax.rem(me_w + WAVE - d, WAVE) if arriving else me_w
        return pltpu.make_async_remote_copy(
            src_ref=a_send.at[c, target],
            dst_ref=a_recv.at[c, place],
            send_sem=a_ssem.at[c, d - 1],
            recv_sem=a_rsem.at[c, d - 1],
            device_id={"wave": target},
            device_id_type=MESH,
        )

    for c in range(CHUNKS):
        spec_load(c).start()
        leaf_load(c).start()
    for l in range(LEVELS):
        lev_load(l).start()
    lat_load().start()

    barrier = pltpu.get_barrier_semaphore()
    for l in range(LEVELS):
        pl.semaphore_signal(barrier, inc=1, device_id={"deg": me_d ^ (1 << l)}, device_id_type=MESH)
    for d in range(1, WAVE):
        pl.semaphore_signal(
            barrier, inc=1, device_id={"wave": lax.rem(me_w + d, WAVE)}, device_id_type=MESH
        )

    def pack(l, c, values):
        s = lax.rem(me_d // (1 << l), 2)
        mask = lane_half == 1 - s
        upper = jnp.broadcast_to(s, (COLS, NODE)) == 1
        for p in range(PAIRS):
            even, odd = values[2 * p], values[2 * p + 1]
            kept = jnp.where(upper, even, odd)
            moved = pltpu.roll(jnp.where(upper, odd, even), NODE // 2, 1)
            send[l, c * PAIRS + p] = jnp.where(mask, kept, moved)

    def leaf(c):
        spec_load(c).wait()
        leaf_load(c).wait()
        degree = lax.broadcasted_iota(jnp.int32, (256, NODE), 0)
        values = []
        for j in range(CHUNK):
            m = c * CHUNK + j
            coef = spec_v[m]
            picks = jnp.where(degree == skel_ref[pl.ds(m, 1), :], 1.0, 0.0).astype(jnp.bfloat16)
            acc = jnp.dot(coef, picks, preferred_element_type=jnp.float32)
            acc = acc + jnp.dot(coef, leaf_v[m], preferred_element_type=jnp.float32)
            values.append(acc.astype(jnp.bfloat16))
        for j in range(CHUNK):
            state[c * CHUNK + j] = values[j]
        pack(0, c, values)

    def combine(l, c):
        level_copy(l, c).wait_recv()
        s = lax.rem(me_d // (1 << l), 2)
        mask = lane_half == s
        upper = jnp.broadcast_to(s, (COLS, NODE)) == 1
        joined = []
        for p in range(PAIRS):
            got = recv[l, c * PAIRS + p]
            turned = pltpu.roll(got, NODE // 2, 1)
            for j, other in (
                (2 * p, jnp.where(upper, got, turned)),
                (2 * p + 1, jnp.where(upper, turned, got)),
            ):
                joined.append(jnp.where(mask, state[c * CHUNK + j], other))
        values = [
            jnp.dot(joined[j], lev_v[l, c * CHUNK + j], preferred_element_type=jnp.float32).astype(
                jnp.bfloat16
            )
            for j in range(CHUNK)
        ]
        if l < LEVELS - 1:
            for j in range(CHUNK):
                state[c * CHUNK + j] = values[j]
            pack(l + 1, c, values)
        return values

    def latitudes(c, values):
        for j in range(CHUNK):
            rows = jnp.dot(values[j], lat_v[c * CHUNK + j], preferred_element_type=jnp.float32)
            real, imag = rows[:32], rows[32:]
            at = pl.ds(c * CHUNK + j, 1)
            co, si = ph_c[at, :], ph_s[at, :]
            lat32[pl.ds(j, 32, stride=2 * CHUNK), :] = real * co + imag * si
            lat32[pl.ds(CHUNK + j, 32, stride=2 * CHUNK), :] = imag * co - real * si
        for w in range(WAVE):
            a_send[c, w] = lat32[w * 64 : (w + 1) * 64, :].astype(jnp.bfloat16)
        for d in (4, 3, 5, 2, 6, 1, 7):
            wave_copy(c, d).start()
        a_recv[c, me_w] = a_send[c, me_w]

    def gathered(pair):
        for k in range(2):
            for d in range(1, WAVE):
                wave_copy(2 * pair + k, d, True).wait_recv()
        lanes = pl.ds(pl.multiple_of(pair * 128, 128), 128)
        for f in range(4):
            block = jnp.concatenate(
                [
                    a_recv[2 * pair + k, :, f * 16 : (f + 1) * 16, :].astype(jnp.float32)
                    for k in range(2)
                ],
                axis=0,
            )
            for r in range(2):
                part = block[:, r * 8 : (r + 1) * 8, :].reshape(128, 128)
                xt_ref[r, f * 128 : (f + 1) * 128, lanes] = part.T.astype(jnp.bfloat16)

    def table(c):
        lanes = lax.broadcasted_iota(jnp.int32, (CHUNK, 128), 1)
        unit = jnp.pi / NLON
        start, turn = [], []
        for w in range(WAVE):
            q = q_v[pl.ds(pl.multiple_of(w * SLOTS + c * CHUNK, 8), CHUNK), :]
            weight = jnp.where(q == 0.0, 1.0, 2.0)
            qi = q.astype(jnp.int32)
            first = lax.rem(qi * (2 * lanes + 1), 2 * NLON).astype(jnp.float32) * unit
            step = lax.rem(qi * 256, 2 * NLON).astype(jnp.float32) * unit
            start += [weight * jnp.cos(first), weight * jnp.sin(first)]
            turn += [jnp.cos(step), jnp.sin(step)]

        def tile(t, carry):
            carry = list(carry)
            for half in range(2):
                lon = slice(half * 128, (half + 1) * 128)
                for w in range(0, WAVE, 2):
                    rows = pl.ds(pl.multiple_of(c * 64 + w * 8, 16), 16)
                    for r in range(2):
                        t_ref[t, r, rows, lon] = jnp.concatenate(
                            [carry[2 * w + r], carry[2 * w + 2 + r]], axis=0
                        ).astype(jnp.bfloat16)
                for w in range(WAVE):
                    co, si = carry[2 * w], carry[2 * w + 1]
                    rc, rs = turn[2 * w], turn[2 * w + 1]
                    carry[2 * w] = co * rc - si * rs
                    carry[2 * w + 1] = si * rc + co * rs
            return tuple(carry)

        lax.fori_loop(0, LON_TILES, tile, tuple(start))

    def early(at):
        def group(g, _):
            for k in range(EARLY):
                t = at + g * EARLY + k
                for r in range(2):
                    part_ref[t, r] = jnp.dot(
                        xt_ref[r, :, :256], t_ref[t, r, :256], preferred_element_type=jnp.float32
                    )
            return 0

        lax.fori_loop(0, LON_TILES // 2 // EARLY, group, 0)

    leaf(0)
    for g in range(4):
        row = wm_ref[g : g + 1, :].astype(jnp.float32)
        q_v[g * 128 : (g + 1) * 128, :] = jnp.broadcast_to(row, (128, 128)).T
    phase = q_v[pl.ds(pl.multiple_of(me_w * SLOTS, 8), SLOTS), :] * (jnp.pi / NLON)
    ph_c[...] = jnp.cos(phase)
    ph_s[...] = jnp.sin(phase)
    pl.semaphore_wait(barrier, LEVELS + WAVE - 1)
    level_copy(0, 0).start()

    offsets = [0]
    for d in DELAY:
        offsets.append(offsets[-1] + d)

    def active(t, k):
        return jnp.logical_and(t >= offsets[k], t < offsets[k] + CHUNKS)

    def step(t, _):
        @pl.when(jnp.logical_and(t >= 1, t < CHUNKS))
        def _():
            leaf(t)
            level_copy(0, t).start()

        @pl.when(active(t, 1))
        def _():
            c = t - offsets[1]

            @pl.when(c == 0)
            def _():
                lev_load(0).wait()

            combine(0, c)
            level_copy(1, c).start()

        @pl.when(active(t, 2))
        def _():
            c = t - offsets[2]

            @pl.when(c == 0)
            def _():
                lev_load(1).wait()

            combine(1, c)
            level_copy(2, c).start()

        @pl.when(active(t, 3))
        def _():
            c = t - offsets[3]

            @pl.when(c == 0)
            def _():
                lev_load(2).wait()
                lat_load().wait()

            latitudes(c, combine(2, c))

        @pl.when(active(t, 4))
        def _():
            c = t - offsets[4]

            @pl.when(lax.rem(c, 2) == 1)
            def _():
                gathered(c // 2)

        @pl.when(t < CHUNKS)
        def _():
            table(t)

        @pl.when(t == offsets[3] + CHUNKS - 1)
        def _():
            early(0)
            early(LON_TILES // 2)

        return 0

    lax.fori_loop(0, CHUNKS + offsets[4], step, 0)

    def drain(c, _):
        for l in range(LEVELS):
            level_copy(l, c).wait_send()
        for d in range(1, WAVE):
            wave_copy(c, d).wait_send()
        return 0

    lax.fori_loop(0, CHUNKS, drain, 0)


def dft_kernel(xt_ref, t_ref, part_ref, out_hbm, low, high, low_sem, high_sem):
    def copies(t, slot):
        near = pl.ds(pl.multiple_of(t * LON_TILE, LON_TILE), LON_TILE)
        far = pl.ds(pl.multiple_of((2 * LON_TILES - 1 - t) * LON_TILE, LON_TILE), LON_TILE)
        return (
            pltpu.make_async_copy(low.at[slot], out_hbm.at[:, near], low_sem.at[slot]),
            pltpu.make_async_copy(high.at[slot], out_hbm.at[:, far], high_sem.at[slot]),
        )

    mirror = 127 - lax.broadcasted_iota(jnp.int32, (512, 128), 1)

    def group(g, _):
        for k in range(UNROLL):
            t = g * UNROLL + k

            @pl.when(g > 0)
            def _():
                for copy in copies(t - UNROLL, k):
                    copy.wait()

        for k in range(UNROLL):
            t = g * UNROLL + k
            even, odd = (
                part_ref[t, r]
                + jnp.dot(
                    xt_ref[r, :, 256:], t_ref[t, r, 256:], preferred_element_type=jnp.float32
                )
                for r in range(2)
            )
            low[k] = (even - odd).astype(jnp.bfloat16)
            total = even + odd
            for h in range(2):
                high[k, :, h * 128 : (h + 1) * 128] = jnp.take_along_axis(
                    total[:, (1 - h) * 128 : (2 - h) * 128], mirror, axis=1
                ).astype(jnp.bfloat16)
            for copy in copies(t, k):
                copy.start()
        return 0

    lax.fori_loop(0, LON_TILES // UNROLL, group, 0)
    for k in range(UNROLL):
        for copy in copies(LON_TILES - UNROLL + k, k):
            copy.wait()


def body(spectrum, leaf_map, level_maps, lat_map, skeleton, wavemap):
    any_spec = pl.BlockSpec(memory_space=pltpu.HBM)
    vmem_spec = pl.BlockSpec(memory_space=pltpu.VMEM)
    bf16, f32 = jnp.bfloat16, jnp.float32
    dma = pltpu.SemaphoreType.DMA
    xt, table, part = pl.pallas_call(
        comm_kernel,
        out_shape=(
            pltpu.VMEM((2, 512, 512), bf16),
            pltpu.VMEM((LON_TILES, 2, 512, LON_TILE), bf16),
            pltpu.VMEM((LON_TILES, 2, 512, LON_TILE), f32),
        ),
        in_specs=[any_spec] * 4 + [vmem_spec] * 2,
        out_specs=(vmem_spec,) * 3,
        scratch_shapes=[
            pltpu.VMEM((SLOTS, COLS, 256), bf16),
            pltpu.VMEM((SLOTS, 256, NODE), bf16),
            pltpu.VMEM((LEVELS, SLOTS, NODE, NODE), bf16),
            pltpu.VMEM((SLOTS, NODE, NODE), bf16),
            pltpu.VMEM((SLOTS, COLS, NODE), bf16),
            pltpu.VMEM((LEVELS, SLOTS // 2, COLS, NODE), bf16),
            pltpu.VMEM((LEVELS, SLOTS // 2, COLS, NODE), bf16),
            pltpu.VMEM((CHUNK * COLS, NODE), f32),
            pltpu.VMEM((CHUNKS, WAVE, 64, NODE), bf16),
            pltpu.VMEM((CHUNKS, WAVE, 64, NODE), bf16),
            pltpu.VMEM((512, 128), f32),
            pltpu.VMEM((SLOTS, 128), f32),
            pltpu.VMEM((SLOTS, 128), f32),
            dma((CHUNKS,)),
            dma((CHUNKS,)),
            dma((LEVELS,)),
            dma((1,)),
            dma((LEVELS, CHUNKS)),
            dma((LEVELS, CHUNKS)),
            dma((CHUNKS, WAVE - 1)),
            dma((CHUNKS, WAVE - 1)),
        ],
        compiler_params=pltpu.CompilerParams(
            collective_id=0, has_side_effects=True, vmem_limit_bytes=VMEM_FIRST * 1024 * 1024
        ),
    )(
        spectrum.reshape(SLOTS, COLS, 256),
        leaf_map,
        level_maps,
        lat_map,
        skeleton,
        wavemap.reshape(4, 128),
    )
    grid = pl.pallas_call(
        dft_kernel,
        out_shape=jax.ShapeDtypeStruct((512, NLON), bf16),
        in_specs=[vmem_spec] * 3,
        out_specs=any_spec,
        scratch_shapes=[
            pltpu.VMEM((UNROLL, 512, LON_TILE), bf16),
            pltpu.VMEM((UNROLL, 512, LON_TILE), bf16),
            dma((UNROLL,)),
            dma((UNROLL,)),
        ],
        compiler_params=pltpu.CompilerParams(vmem_limit_bytes=VMEM_SECOND * 1024 * 1024),
    )(xt, table, part)
    return grid.reshape(4, 128, NLON)


def solution(mesh):
    placed = (
        P("wave", None, None, "deg"),
        P("wave", "deg", None),
        P(None, "wave", "deg", None),
        P("wave", None, "deg"),
        P("wave", "deg"),
        P(),
    )
    return jax.shard_map(
        body, mesh=mesh, in_specs=placed, out_specs=P("wave", "deg", None), check_vma=False
    )
```
